32 devices in a mesh: row: 8 (over z, y), col: 4 (over x, core).
Axes of the slice: x: 2, y: 2, z: 4, core: 2. Of those that a mesh axis runs over, the one named last changes fastest.
Arguments:
- eigvecs: bfloat16 [131072, 4096], P('row', 'col'), may hold values from -6 to 6
- reflectors: bfloat16 [131072, 1024], P('row', 'col'), may hold values from -0.046875 to 0.046875
- t_factors: float32 [1024, 256], P('col'), as said below
- owners: int32 [2], replicated, may hold values from 0 to 3, as said below
- band_owner: int32 [1024, 1], P('row'), may hold values from 0 to 7; in each aligned block of 128 rows (0 to 127, 128 to 255, ...) at most 20 rows name the same one
Outputs:
- owned: bfloat16 [163840, 4096], P('row', 'col')
The draws below stay inside these ranges and needn't reach their ends.
Inputs may be any that keep to these rules, and one draw needn't show every extreme that they name: `owners`: the 2 entries are different column indices, and one of them is the last column index. `t_factors`: each block of 256 rows is upper triangular. `band_owner`: among the 128 rows of one index of row, no owner is named more than 20 times.
All inputs are finite; a program needn't handle non-finite values.
Results may differ from the reference program's by a relative error of at most 0.015.
Values may be sent and summed in bfloat16 or wider, within the bound.
No kernel may reach another device: no remote copies, remote signals or barrier semaphores. Data moves between devices by JAX's collectives and lax.ppermute only.
A program may use at most 384 MiB of HBM per device.

```python
import math
import jax
import jax.numpy as jnp
import numpy as np
from jax import lax

N = 131072
K = 4096
NB = 256
BLKS_DEV = 128
NBLK = 1024
MOST = 20
N_ROW = 8
N_COL = 4


def draw_owners(key, part):
    other_key = jax.random.fold_in(key, 5)
    order_key = jax.random.fold_in(key, 7)
    other = jax.random.randint(other_key, (), 0, N_COL - 1, dtype=jnp.int32)
    flipped = jax.random.randint(order_key, (), 0, 2, dtype=jnp.int32)
    last_index = jnp.int32(N_COL - 1)
    first = jnp.where(flipped == 1, last_index, other)
    second = jnp.where(flipped == 1, other, last_index)
    return jnp.stack([first, second]).astype(jnp.int32)


def draw_t_factors(key, part):
    first_key = jax.random.fold_in(key, 11)
    second_key = jax.random.fold_in(key, 23)
    shape_all = (N_COL * NB, NB)
    upper_part = jax.random.normal(first_key, shape_all, jnp.float32) / jnp.sqrt(jnp.float32(NB))
    diagonal_part = jax.random.uniform(second_key, shape_all, jnp.float32, 1.0, 2.0)
    local_row = jnp.arange(N_COL * NB, dtype=jnp.int32)[:, None] % NB
    column_id = jnp.arange(NB, dtype=jnp.int32)[None, :]
    result = jnp.where(column_id > local_row, upper_part, 0.0)
    result = jnp.where(column_id == local_row, diagonal_part, result)
    return result.astype(jnp.float32)


def shard_levels(own_key, shape, pieces, low, high):
    gain, own = 1.0, jax.random.fold_in(own_key, 6)
    for dim, shards_of in pieces:
        steps = jnp.exp(jax.random.uniform(jax.random.fold_in(own, dim), (shards_of,), jnp.float32, low / len(pieces), high / len(pieces)))
        gain = gain * jnp.repeat(steps, shape[dim] // shards_of).reshape([-1 if axis == dim else 1 for axis in range(len(shape))])
    return gain


def shared_out(rng, own, number, rows, number_of, top, most, lean):
    sequence = jax.random.permutation(rng, number_of)
    crowded, ordinary = shares(number_of, rows * top, most, lean, True), shares(number_of, rows * top, most, lean, False)
    places = jnp.arange(number_of)

    def named(sizes, offset_by):
        used = int((sizes > 0).sum())
        fixed = max(1, used // 4)
        shifted = fixed + (places - fixed + offset_by * (used - fixed)) % max(1, number_of - fixed)
        return jnp.zeros((number_of,), jnp.int32).at[sequence[jnp.where(places < fixed, places, shifted)]].set(jnp.asarray(sizes, jnp.int32))

    sizes = jnp.where(number % 4 == 0, named(crowded, number // 4), named(ordinary, number - number // 4 - 1))
    mixed = jax.random.permutation(jax.random.fold_in(own, 3), number_of)
    source_of, taker = mixed[0:number_of // 2 * 2:2], mixed[1:number_of // 2 * 2:2]
    room = jnp.minimum(sizes[source_of] - 1, most - sizes[taker]) // 2
    room = jnp.where((source_of == sequence[0]) | (taker == sequence[0]) | (sizes[taker] == 0), 0, jnp.maximum(room, 0))
    shifted = jax.random.randint(jax.random.fold_in(own, 4), (number_of // 2,), 0, 1 << 20) % (room + 1)
    sizes = sizes.at[source_of].add(-shifted).at[taker].add(shifted)
    items = jnp.searchsorted(jnp.cumsum(sizes), jnp.arange(rows * top), side="right").astype(jnp.int32)
    table = items.reshape(top, rows).T
    table = table[jax.random.permutation(jax.random.fold_in(own, 1), rows)]
    offset_by = jax.random.randint(jax.random.fold_in(own, 2), (rows, 1), 0, top)
    return jnp.take_along_axis(table, (jnp.arange(top)[None, :] + offset_by) % top, axis=1)


def shares(count, total, reach, slope, full):
    loads = [(1 << 20) // math.isqrt(standing ** slope) + 1 for standing in range(1, count + 1)]
    largest = reach if full else min(reach, max(-(-total // count), total * loads[0] // sum(loads)))
    least = 1 if total - largest >= count - 1 else 0
    holding, rest = [largest] + [least] * (count - 1), total - largest - least * (count - 1)
    while rest > 0:
        movable = [i for i in range(1, count) if holding[i] < largest] or [i for i in range(1, count) if holding[i] < reach]
        whole, left = sum([loads[i] for i in movable]), rest
        for i in movable:
            addition = min(reach - holding[i], max(1, left * loads[i] // whole), rest)
            holding[i] = holding[i] + addition
            rest = rest - addition
    return np.array(holding)


def scatter_about(rng, dims, spread, most, cuts=(), kind=jnp.bfloat16):
    array = jax.random.normal(rng, dims, jnp.float32) * spread
    if len(cuts) > 0:
        array = shard_levels(rng, dims, cuts, -0.22, 0.18) * array
    return jnp.clip(array, min=-most, max=most).astype(kind)


def setup_inputs(seed: int = 0) -> dict:
    splits = jax.random.split(jax.random.key(seed), 6)
    eigvecs = scatter_about(splits[0], (N, K), 1.0, 6.0, ((0, 8), (1, 4)))
    reflectors = scatter_about(splits[1], (N, N_COL * NB), (N // 8) ** -0.5, 0.046875, ((0, 8), (1, 4)))
    t_factors = draw_t_factors(jax.random.fold_in(splits[5], 71), 0)
    owners = draw_owners(jax.random.fold_in(splits[5], 71), 0)
    band_owner_keys = jax.random.split(jax.random.fold_in(splits[4], 1), NBLK // BLKS_DEV)
    band_owner_turns = jax.random.permutation(jax.random.fold_in(splits[4], 3), NBLK // BLKS_DEV)
    band_owner = jax.vmap(lambda own, number: shared_out(jax.random.fold_in(splits[4], 2), own, number, BLKS_DEV, N_ROW, 1, MOST, 2))(band_owner_keys, band_owner_turns).reshape((NBLK, 1))
    return dict(eigvecs=eigvecs, reflectors=reflectors, t_factors=t_factors, owners=owners, band_owner=band_owner)


def apply_columns(column_block, panel_list, triangle_list):
    field = column_block.astype(jnp.float32)
    for which in range(2):
        vectors = panel_list[which].astype(jnp.float32)
        products = jnp.dot(vectors.T, field, precision=lax.Precision.HIGHEST)
        update = jnp.dot(triangle_list[which], products, precision=lax.Precision.HIGHEST).astype(jnp.bfloat16)
        field = field - jnp.dot(vectors, update.astype(jnp.float32), precision=lax.Precision.HIGHEST)
    return field.astype(jnp.bfloat16)


def reference(eigvecs, reflectors, t_factors, owners, band_owner):
    panel_list = [lax.dynamic_slice_in_dim(reflectors, (owners[which] * NB).astype(jnp.int32), NB, 1) for which in range(2)]
    triangle_list = [lax.dynamic_slice_in_dim(t_factors, (owners[which] * NB).astype(jnp.int32), NB, 0) for which in range(2)]
    owner_of = band_owner[:, 0].reshape(N_ROW, BLKS_DEV)
    position = jnp.arange(BLKS_DEV, dtype=jnp.int32)
    shared = (owner_of[:, :, None] == owner_of[:, None, :]) & (position[None, None, :] < position[None, :, None])
    order_in = jnp.sum(shared.astype(jnp.int32), axis=2)
    sources = jnp.arange(N_ROW, dtype=jnp.int32)[:, None]
    target = (owner_of * N_ROW + sources) * MOST + order_in
    target = target.reshape(NBLK).astype(jnp.int32)
    width = K // N_COL

    def one_column(index):
        column_block = lax.dynamic_slice_in_dim(eigvecs, (index * width).astype(jnp.int32), width, 1)
        finished = apply_columns(column_block, panel_list, triangle_list)
        empty_slots = jnp.zeros((N_ROW * N_ROW * MOST, 128, width), jnp.bfloat16)
        return empty_slots.at[target].set(finished.reshape(NBLK, 128, width))

    stacked = lax.map(one_column, jnp.arange(N_COL, dtype=jnp.int32))
    return jnp.transpose(stacked, (1, 2, 0, 3)).reshape(N_ROW * N_ROW * MOST * 128, K)
```

```python
import functools

import jax
import jax.numpy as jnp
from jax import lax
from jax.experimental import pallas as pl
from jax.experimental.pallas import tpu as pltpu
from jax.sharding import PartitionSpec as P


ROWS = 128
contract_rows = (((0,), (0,)), ((), ()))


def broadcast(value, axis, source):
    kept = jnp.where(lax.axis_index(axis) == source, value, 0).astype(value.dtype)
    return lax.psum(kept, axis)


def swap(value, row_count, distance):
    return lax.ppermute(value, "row", [(s, s ^ distance) for s in range(row_count)])


def pieces(total, size):
    return [(at, min(size, total - at)) for at in range(0, total, size)]


def gather_kernel(groups, count, block_ref, filled_ref, source, *rest):
    outs, (stage, in_sems, out_sems) = rest[:groups], rest[groups:]

    def inward(k):
        return pltpu.make_async_copy(source.at[block_ref[k]], stage.at[k], in_sems.at[k])

    def fetch(k, carry):
        @pl.when(filled_ref[k] > 0)
        def _():
            inward(k).start()

        return carry

    lax.fori_loop(0, groups * count, fetch, 0)
    for group in range(groups):

        def send(item, carry):
            k = group * count + item

            @pl.when(filled_ref[k] > 0)
            def _():
                inward(k).wait()

            @pl.when(filled_ref[k] <= 0)
            def _():
                stage[k] = jnp.zeros(stage.shape[1:], stage.dtype)

            pltpu.make_async_copy(stage.at[k], outs[group].at[item], out_sems.at[k]).start()
            return carry

        lax.fori_loop(0, count, send, 0)
    for group in range(groups):

        def drain(item, carry):
            k = group * count + item
            pltpu.make_async_copy(stage.at[k], outs[group].at[item], out_sems.at[k]).wait()
            return carry

        lax.fori_loop(0, count, drain, 0)


def gather_blocks(source, blocks, filled, groups, count):
    any_spec = pl.BlockSpec(memory_space=pl.ANY)
    smem_spec = pl.BlockSpec(memory_space=pltpu.SMEM)
    out = jax.ShapeDtypeStruct((count,) + source.shape[1:], source.dtype)
    total = groups * count
    return pl.pallas_call(
        functools.partial(gather_kernel, groups, count),
        out_shape=[out] * groups,
        in_specs=[smem_spec, smem_spec, any_spec],
        out_specs=[any_spec] * groups,
        scratch_shapes=[
            pltpu.VMEM((total,) + source.shape[1:], source.dtype),
            pltpu.SemaphoreType.DMA((total,)),
            pltpu.SemaphoreType.DMA((total,)),
        ],
        compiler_params=pltpu.CompilerParams(vmem_limit_bytes=56 * 2**20),
    )(blocks, filled, source)


def finish_kernel(groups, count, block_ref, filled_ref, base_ref, z_ref, a_ref, b_ref, y_ref, *outs):
    depth = a_ref.shape[-1]
    step = pl.program_id(0)
    value = z_ref[...].astype(jnp.float32)
    value = value - jnp.dot(a_ref[...], y_ref[:depth, :], preferred_element_type=jnp.float32)
    value = value - jnp.dot(b_ref[...], y_ref[depth:, :], preferred_element_type=jnp.float32)
    value = jnp.where(filled_ref[step] > 0, value, 0.0).astype(outs[0].dtype)
    for group in range(groups):

        @pl.when(step // count == group)
        def _():
            outs[group][...] = value


def finish_here(z, a, b, y, blocks, filled, groups, count, base=None, slot_total=None):
    width, depth = z.shape[2], a.shape[2]
    pick = lambda i, block_ref, *_: (block_ref[i], 0, 0)

    def out_spec(group):
        if base is not None:
            return pl.BlockSpec((None, ROWS, width), lambda i, block_ref, filled_ref, base_ref: (base_ref[0] + i, 0, 0))
        return pl.BlockSpec((None, ROWS, width), lambda i, *_: (jnp.clip(i - group * count, 0, count - 1), 0, 0))

    length = count if slot_total is None else slot_total
    return pl.pallas_call(
        functools.partial(finish_kernel, groups, count),
        grid_spec=pltpu.PrefetchScalarGridSpec(
            num_scalar_prefetch=3,
            grid=(groups * count,),
            in_specs=[
                pl.BlockSpec((None, ROWS, width), pick),
                pl.BlockSpec((None, ROWS, depth), pick),
                pl.BlockSpec((None, ROWS, depth), pick),
                pl.BlockSpec(y.shape, lambda i, *_: (0, 0)),
            ],
            out_specs=[out_spec(group) for group in range(groups)],
        ),
        out_shape=[jax.ShapeDtypeStruct((length, ROWS, width), z.dtype)] * groups,
    )(blocks, filled, jnp.zeros((1,), jnp.int32) if base is None else base.reshape(1), z, a, b, y)


def settle_kernel(groups, count, slot_ref, owned_ref, *refs):
    z_refs, (v_ref, y_ref, out_ref) = refs[:groups], refs[groups:]
    parts, depth = v_ref.shape[0], v_ref.shape[-1]
    for group in range(groups):

        @pl.when(pl.program_id(0) // count == group)
        def _():
            value = z_refs[group][...].astype(jnp.float32)
            for part in range(parts):
                value = value - jnp.dot(
                    v_ref[part], y_ref[part * depth : (part + 1) * depth, :], preferred_element_type=jnp.float32
                )
            out_ref[...] = value.astype(out_ref.dtype)


def settle_there(owned, z_list, v, y, first, stride, slots):
    groups, count, width = len(z_list), z_list[0].shape[0], owned.shape[2]
    parts, depth = v.shape[0], v.shape[3]

    def z_spec(group):
        return pl.BlockSpec((None, ROWS, width), lambda i, slot_ref: (jnp.clip(i - group * count, 0, count - 1), 0, 0))

    return pl.pallas_call(
        functools.partial(settle_kernel, groups, count),
        grid_spec=pltpu.PrefetchScalarGridSpec(
            num_scalar_prefetch=1,
            grid=(groups * count,),
            in_specs=[pl.BlockSpec(memory_space=pl.ANY)]
            + [z_spec(group) for group in range(groups)]
            + [
                pl.BlockSpec(
                    (parts, None, ROWS, depth),
                    lambda i, slot_ref: (0, (i // count) * stride + first + i % count, 0, 0),
                ),
                pl.BlockSpec(y.shape, lambda i, slot_ref: (0, 0)),
            ],
            out_specs=pl.BlockSpec((None, ROWS, width), lambda i, slot_ref: (slot_ref[i], 0, 0)),
        ),
        out_shape=jax.ShapeDtypeStruct(owned.shape, owned.dtype),
        input_output_aliases={1: 0},
    )(slots, owned, *z_list, v, y)


def body(eigvecs, reflectors, t_factors, owners, band_owner):
    row_count, col_count = lax.axis_size("row"), lax.axis_size("col")
    me, col = lax.axis_index("row"), lax.axis_index("col")
    block_count = eigvecs.shape[0] // ROWS
    width = eigvecs.shape[1]
    depth = reflectors.shape[1]
    capacity = (5 * block_count + 4 * row_count - 1) // (4 * row_count)
    slot_total = row_count * capacity
    early = 7 * capacity // 10
    share = 2 * depth // col_count
    half = row_count // 2
    order = list(range(half // 2, half)) + list(range(half, row_count)) + list(range(1, half // 2))
    early_parts = [(0, max(1, early // 6))]
    early_parts += [(early_parts[0][1], early - early_parts[0][1])]
    late_parts = [(early + at, count) for at, count in pieces(capacity - early, 4)]

    owner_of = band_owner[:, 0]
    position = jnp.arange(block_count, dtype=jnp.int32)
    shared = (owner_of[:, None] == owner_of[None, :]) & (position[None, :] < position[:, None])
    order_in = jnp.sum(shared.astype(jnp.int32), axis=1)
    slot_index = owner_of * capacity + order_in
    hits = (slot_index[None, :] == jnp.arange(slot_total, dtype=jnp.int32)[:, None]).astype(jnp.int32)
    slot_table = jnp.stack([jnp.sum(hits * position[None, :], axis=1), jnp.sum(hits, axis=1)])

    def tables(at, count):
        starts = [(me ^ d) * capacity + at for d in order]
        both = jnp.concatenate([lax.dynamic_slice(slot_table, (0, s), (2, count)) for s in starts], axis=1)
        return both[0], both[1]

    z = eigvecs.reshape(block_count, ROWS, width)

    raw = {}
    for at, count in early_parts:
        packed = gather_blocks(z, *tables(at, count), len(order), count)
        raw[at] = [swap(item, row_count, d) for d, item in zip(order, packed)]

    panels = [broadcast(reflectors, "col", owners[which]) for which in range(2)]
    mine = jnp.concatenate([jnp.where(col == owners[which], t_factors, 0.0) for which in range(2)], axis=0)
    triangles = lax.psum(mine, "col")

    partial_value = jnp.concatenate(
        [
            lax.dot_general(panel, eigvecs, contract_rows, preferred_element_type=jnp.float32)
            for panel in panels
        ],
        axis=0,
    )
    products = lax.psum(partial_value.astype(jnp.bfloat16), "row").astype(jnp.float32)
    gram = lax.psum(
        lax.dot_general(panels[1], panels[0], contract_rows, preferred_element_type=jnp.float32), "row"
    )
    first = jnp.dot(triangles[:depth], products[:depth], precision=lax.Precision.HIGHEST).astype(jnp.bfloat16)
    rest = products[depth:] - jnp.dot(gram, first.astype(jnp.float32), precision=lax.Precision.HIGHEST)
    second = jnp.dot(triangles[depth:], rest, precision=lax.Precision.HIGHEST).astype(jnp.bfloat16)
    update = jnp.concatenate([first, second], axis=0)

    both = jnp.concatenate(panels, axis=1)
    slim = lax.dynamic_slice(both, (0, col * share), (both.shape[0], share)).reshape(block_count, ROWS, share)
    slim_packed = gather_blocks(slim, *tables(0, early), len(order), early)
    slim_list = [swap(item, row_count, d) for d, item in zip(order, slim_packed)]

    v0 = panels[0].reshape(block_count, ROWS, depth)
    v1 = panels[1].reshape(block_count, ROWS, depth)

    late = {}
    for at, count in late_parts:
        done = finish_here(z, v0, v1, update, *tables(at, count), len(order), count)
        late[at] = [swap(item, row_count, d) for d, item in zip(order, done)]

    slim_list, _ = lax.optimization_barrier((slim_list, done))
    wide_there = lax.all_gather(jnp.concatenate(slim_list, axis=0), "col", axis=0)

    mine = lax.dynamic_slice(slot_table, (0, me * capacity), (2, capacity))
    (owned,) = finish_here(z, v0, v1, update, mine[0], mine[1], 1, capacity, me * capacity, slot_total)
    for at, count in early_parts:
        slots = jnp.concatenate([(me ^ d) * capacity + at + jnp.arange(count, dtype=jnp.int32) for d in order])
        owned = settle_there(owned, raw[at], wide_there, update, at, early, slots)
    for at, count in late_parts:
        for d, item in zip(order, late[at]):
            owned = lax.dynamic_update_slice(owned, item, ((me ^ d) * capacity + at, 0, 0))
    return owned.reshape(slot_total * ROWS, width)


def solution(mesh):
    in_specs = (P("row", "col"), P("row", "col"), P("col", None), P(), P("row", None))
    out_specs = P("row", "col")
    return jax.shard_map(body, mesh=mesh, in_specs=in_specs, out_specs=out_specs, check_vma=False)
```

```python
import functools

import jax
import jax.numpy as jnp
from jax import lax
from jax.experimental import pallas as pl
from jax.experimental.pallas import tpu as pltpu
from jax.sharding import PartitionSpec as P


ROWS = 128
contract_rows = (((0,), (0,)), ((), ()))


def swap(value, row_count, distance):
    return lax.ppermute(value, "row", [(s, s ^ distance) for s in range(row_count)])


def pieces(total, size):
    return [(at, min(size, total - at)) for at in range(0, total, size)]


def gather_kernel(groups, count, block_ref, filled_ref, source, *rest):
    outs, (stage, in_sems, out_sems) = rest[:groups], rest[groups:]

    def inward(k):
        return pltpu.make_async_copy(source.at[block_ref[k]], stage.at[k], in_sems.at[k])

    def fetch(k, carry):
        @pl.when(filled_ref[k] > 0)
        def _():
            inward(k).start()

        return carry

    lax.fori_loop(0, groups * count, fetch, 0)
    for group in range(groups):

        def send(item, carry):
            k = group * count + item

            @pl.when(filled_ref[k] > 0)
            def _():
                inward(k).wait()

            @pl.when(filled_ref[k] <= 0)
            def _():
                stage[k] = jnp.zeros(stage.shape[1:], stage.dtype)

            pltpu.make_async_copy(stage.at[k], outs[group].at[item], out_sems.at[k]).start()
            return carry

        lax.fori_loop(0, count, send, 0)
    for group in range(groups):

        def drain(item, carry):
            k = group * count + item
            pltpu.make_async_copy(stage.at[k], outs[group].at[item], out_sems.at[k]).wait()
            return carry

        lax.fori_loop(0, count, drain, 0)


def gather_blocks(source, blocks, filled, groups, count):
    any_spec = pl.BlockSpec(memory_space=pl.ANY)
    smem_spec = pl.BlockSpec(memory_space=pltpu.SMEM)
    out = jax.ShapeDtypeStruct((count,) + source.shape[1:], source.dtype)
    total = groups * count
    return pl.pallas_call(
        functools.partial(gather_kernel, groups, count),
        out_shape=[out] * groups,
        in_specs=[smem_spec, smem_spec, any_spec],
        out_specs=[any_spec] * groups,
        scratch_shapes=[
            pltpu.VMEM((total,) + source.shape[1:], source.dtype),
            pltpu.SemaphoreType.DMA((total,)),
            pltpu.SemaphoreType.DMA((total,)),
        ],
        compiler_params=pltpu.CompilerParams(vmem_limit_bytes=56 * 2**20),
    )(blocks, filled, source)


def finish_kernel(groups, count, block_ref, filled_ref, base_ref, z_ref, a_ref, b_ref, y_ref, *outs):
    depth = a_ref.shape[-1]
    step = pl.program_id(0)
    value = z_ref[...].astype(jnp.float32)
    value = value - jnp.dot(a_ref[...], y_ref[:depth, :], preferred_element_type=jnp.float32)
    value = value - jnp.dot(b_ref[...], y_ref[depth:, :], preferred_element_type=jnp.float32)
    value = jnp.where(filled_ref[step] > 0, value, 0.0).astype(outs[0].dtype)
    for group in range(groups):

        @pl.when(step // count == group)
        def _():
            outs[group][...] = value


def finish_here(z, a, b, y, blocks, filled, groups, count, base=None, slot_total=None):
    width, depth = z.shape[2], a.shape[2]
    pick = lambda i, block_ref, *_: (block_ref[i], 0, 0)

    def out_spec(group):
        if base is not None:
            return pl.BlockSpec((None, ROWS, width), lambda i, block_ref, filled_ref, base_ref: (base_ref[0] + i, 0, 0))
        return pl.BlockSpec((None, ROWS, width), lambda i, *_: (jnp.clip(i - group * count, 0, count - 1), 0, 0))

    length = count if slot_total is None else slot_total
    return pl.pallas_call(
        functools.partial(finish_kernel, groups, count),
        grid_spec=pltpu.PrefetchScalarGridSpec(
            num_scalar_prefetch=3,
            grid=(groups * count,),
            in_specs=[
                pl.BlockSpec((None, ROWS, width), pick),
                pl.BlockSpec((None, ROWS, depth), pick),
                pl.BlockSpec((None, ROWS, depth), pick),
                pl.BlockSpec(y.shape, lambda i, *_: (0, 0)),
            ],
            out_specs=[out_spec(group) for group in range(groups)],
        ),
        out_shape=[jax.ShapeDtypeStruct((length, ROWS, width), z.dtype)] * groups,
    )(blocks, filled, jnp.zeros((1,), jnp.int32) if base is None else base.reshape(1), z, a, b, y)


def settle_kernel(groups, count, slot_ref, owned_ref, *refs):
    z_refs, (v_ref, y_ref, out_ref) = refs[:groups], refs[groups:]
    parts, depth = v_ref.shape[0], v_ref.shape[-1]
    for group in range(groups):

        @pl.when(pl.program_id(0) // count == group)
        def _():
            value = z_refs[group][...].astype(jnp.float32)
            for part in range(parts):
                value = value - jnp.dot(
                    v_ref[part], y_ref[part * depth : (part + 1) * depth, :], preferred_element_type=jnp.float32
                )
            out_ref[...] = value.astype(out_ref.dtype)


def settle_there(owned, z_list, v, y, first, stride, slots):
    groups, count, width = len(z_list), z_list[0].shape[0], owned.shape[2]
    parts, depth = v.shape[0], v.shape[3]

    def z_spec(group):
        return pl.BlockSpec((None, ROWS, width), lambda i, slot_ref: (jnp.clip(i - group * count, 0, count - 1), 0, 0))

    return pl.pallas_call(
        functools.partial(settle_kernel, groups, count),
        grid_spec=pltpu.PrefetchScalarGridSpec(
            num_scalar_prefetch=1,
            grid=(groups * count,),
            in_specs=[pl.BlockSpec(memory_space=pl.ANY)]
            + [z_spec(group) for group in range(groups)]
            + [
                pl.BlockSpec(
                    (parts, None, ROWS, depth),
                    lambda i, slot_ref: (0, (i // count) * stride + first + i % count, 0, 0),
                ),
                pl.BlockSpec(y.shape, lambda i, slot_ref: (0, 0)),
            ],
            out_specs=pl.BlockSpec((None, ROWS, width), lambda i, slot_ref: (slot_ref[i], 0, 0)),
        ),
        out_shape=jax.ShapeDtypeStruct(owned.shape, owned.dtype),
        input_output_aliases={1: 0},
    )(slots, owned, *z_list, v, y)


def body(eigvecs, reflectors, t_factors, owners, band_owner):
    row_count, col_count = lax.axis_size("row"), lax.axis_size("col")
    me, col = lax.axis_index("row"), lax.axis_index("col")
    block_count = eigvecs.shape[0] // ROWS
    width = eigvecs.shape[1]
    depth = reflectors.shape[1]
    capacity = (5 * block_count + 4 * row_count - 1) // (4 * row_count)
    slot_total = row_count * capacity
    early = 3 * capacity // 5
    share = 2 * depth // col_count
    half = row_count // 2
    order = list(range(half // 2, half)) + list(range(half, row_count)) + list(range(1, half // 2))
    early_parts = [(0, max(1, early // 6))]
    early_parts += [(early_parts[0][1], early - early_parts[0][1])]
    late_parts = [(early + at, count) for at, count in pieces(capacity - early, max(1, (capacity - early) // 2))]

    owner_of = band_owner[:, 0]
    position = jnp.arange(block_count, dtype=jnp.int32)
    shared = (owner_of[:, None] == owner_of[None, :]) & (position[None, :] < position[:, None])
    order_in = jnp.sum(shared.astype(jnp.int32), axis=1)
    slot_index = owner_of * capacity + order_in
    hits = (slot_index[None, :] == jnp.arange(slot_total, dtype=jnp.int32)[:, None]).astype(jnp.int32)
    slot_table = jnp.stack([jnp.sum(hits * position[None, :], axis=1), jnp.sum(hits, axis=1)])

    def tables(at, count):
        starts = [(me ^ d) * capacity + at for d in order]
        both = jnp.concatenate([lax.dynamic_slice(slot_table, (0, s), (2, count)) for s in starts], axis=1)
        return both[0], both[1]

    z = eigvecs.reshape(block_count, ROWS, width)

    raw = {}
    for at, count in early_parts:
        packed = gather_blocks(z, *tables(at, count), len(order), count)
        raw[at] = [swap(item, row_count, d) for d, item in zip(order, packed)]

    candidates = lax.all_gather(reflectors, "col", axis=0)
    panels = [lax.dynamic_index_in_dim(candidates, owners[which], 0, keepdims=False) for which in range(2)]
    mine = jnp.concatenate([jnp.where(col == owners[which], t_factors, 0.0) for which in range(2)], axis=0)
    triangles = lax.psum(mine, "col")

    partial_value = jnp.concatenate(
        [
            lax.dot_general(panel, eigvecs, contract_rows, preferred_element_type=jnp.float32)
            for panel in panels
        ],
        axis=0,
    )
    gram = lax.dot_general(panels[1], panels[0], contract_rows, preferred_element_type=jnp.float32)
    gram = jnp.concatenate([jnp.zeros_like(gram), gram], axis=0)
    partial_value = jnp.concatenate([partial_value.astype(jnp.bfloat16), gram.astype(jnp.bfloat16)], axis=1)
    totals = lax.psum(partial_value, "row").astype(jnp.float32)
    products, gram = totals[:, :width], totals[depth:, width:]
    first = jnp.dot(triangles[:depth], products[:depth], precision=lax.Precision.HIGHEST).astype(jnp.bfloat16)
    rest = products[depth:] - jnp.dot(gram, first.astype(jnp.float32), precision=lax.Precision.HIGHEST)
    second = jnp.dot(triangles[depth:], rest, precision=lax.Precision.HIGHEST).astype(jnp.bfloat16)
    update = jnp.concatenate([first, second], axis=0)

    both = jnp.concatenate(panels, axis=1)
    slim = lax.dynamic_slice(both, (0, col * share), (both.shape[0], share)).reshape(block_count, ROWS, share)
    slim_packed = gather_blocks(slim, *tables(0, early), len(order), early)
    slim_list = [swap(item, row_count, d) for d, item in zip(order, slim_packed)]

    v0 = panels[0].reshape(block_count, ROWS, depth)
    v1 = panels[1].reshape(block_count, ROWS, depth)

    late = {}
    for at, count in late_parts:
        done = finish_here(z, v0, v1, update, *tables(at, count), len(order), count)
        late[at] = [swap(item, row_count, d) for d, item in zip(order, done)]

    slim_list, _ = lax.optimization_barrier((slim_list, done))
    wide_there = lax.all_gather(jnp.concatenate(slim_list, axis=0), "col", axis=0)

    mine = lax.dynamic_slice(slot_table, (0, me * capacity), (2, capacity))
    (owned,) = finish_here(z, v0, v1, update, mine[0], mine[1], 1, capacity, me * capacity, slot_total)
    for at, count in early_parts:
        slots = jnp.concatenate([(me ^ d) * capacity + at + jnp.arange(count, dtype=jnp.int32) for d in order])
        owned = settle_there(owned, raw[at], wide_there, update, at, early, slots)
    for at, count in late_parts:
        for d, item in zip(order, late[at]):
            owned = lax.dynamic_update_slice(owned, item, ((me ^ d) * capacity + at, 0, 0))
    return owned.reshape(slot_total * ROWS, width)


def solution(mesh):
    in_specs = (P("row", "col"), P("row", "col"), P("col", None), P(), P("row", None))
    out_specs = P("row", "col")
    return jax.shard_map(body, mesh=mesh, in_specs=in_specs, out_specs=out_specs, check_vma=False)
```

```python
import functools

import jax
import jax.numpy as jnp
from jax import lax
from jax.experimental import pallas as pl
from jax.experimental.pallas import tpu as pltpu
from jax.sharding import PartitionSpec as P


ROWS = 128
contract_rows = (((0,), (0,)), ((), ()))


def swap(value, row_count, distance):
    return lax.ppermute(value, "row", [(s, s ^ distance) for s in range(row_count)])


def gather_kernel(groups, count, block_ref, filled_ref, source, *rest):
    outs, (stage, in_sems, out_sems) = rest[:groups], rest[groups:]

    def inward(k):
        return pltpu.make_async_copy(source.at[block_ref[k]], stage.at[k], in_sems.at[k])

    def fetch(k, carry):
        @pl.when(filled_ref[k] > 0)
        def _():
            inward(k).start()

        return carry

    lax.fori_loop(0, groups * count, fetch, 0)
    for group in range(groups):

        def send(item, carry):
            k = group * count + item

            @pl.when(filled_ref[k] > 0)
            def _():
                inward(k).wait()

            @pl.when(filled_ref[k] <= 0)
            def _():
                stage[k] = jnp.zeros(stage.shape[1:], stage.dtype)

            pltpu.make_async_copy(stage.at[k], outs[group].at[item], out_sems.at[k]).start()
            return carry

        lax.fori_loop(0, count, send, 0)
    for group in range(groups):

        def drain(item, carry):
            k = group * count + item
            pltpu.make_async_copy(stage.at[k], outs[group].at[item], out_sems.at[k]).wait()
            return carry

        lax.fori_loop(0, count, drain, 0)


def gather_blocks(source, blocks, filled, groups, count):
    any_spec = pl.BlockSpec(memory_space=pl.ANY)
    smem_spec = pl.BlockSpec(memory_space=pltpu.SMEM)
    out = jax.ShapeDtypeStruct((count,) + source.shape[1:], source.dtype)
    total = groups * count
    return pl.pallas_call(
        functools.partial(gather_kernel, groups, count),
        out_shape=[out] * groups,
        in_specs=[smem_spec, smem_spec, any_spec],
        out_specs=[any_spec] * groups,
        scratch_shapes=[
            pltpu.VMEM((total,) + source.shape[1:], source.dtype),
            pltpu.SemaphoreType.DMA((total,)),
            pltpu.SemaphoreType.DMA((total,)),
        ],
        compiler_params=pltpu.CompilerParams(vmem_limit_bytes=56 * 2**20),
    )(blocks, filled, source)


def finish_kernel(groups, count, block_ref, filled_ref, base_ref, z_ref, a_ref, b_ref, y_ref, *outs):
    depth = a_ref.shape[-1]
    step = pl.program_id(0)
    value = z_ref[...].astype(jnp.float32)
    value = value - jnp.dot(a_ref[...], y_ref[:depth, :], preferred_element_type=jnp.float32)
    value = value - jnp.dot(b_ref[...], y_ref[depth:, :], preferred_element_type=jnp.float32)
    value = jnp.where(filled_ref[step] > 0, value, 0.0).astype(outs[0].dtype)
    for group in range(groups):

        @pl.when(step // count == group)
        def _():
            outs[group][...] = value


def finish_here(z, a, b, y, blocks, filled, groups, count, base=None, slot_total=None):
    width, depth = z.shape[2], a.shape[2]
    pick = lambda i, block_ref, *_: (block_ref[i], 0, 0)

    def out_spec(group):
        if base is not None:
            return pl.BlockSpec((None, ROWS, width), lambda i, block_ref, filled_ref, base_ref: (base_ref[0] + i, 0, 0))
        return pl.BlockSpec((None, ROWS, width), lambda i, *_: (jnp.clip(i - group * count, 0, count - 1), 0, 0))

    length = count if slot_total is None else slot_total
    return pl.pallas_call(
        functools.partial(finish_kernel, groups, count),
        grid_spec=pltpu.PrefetchScalarGridSpec(
            num_scalar_prefetch=3,
            grid=(groups * count,),
            in_specs=[
                pl.BlockSpec((None, ROWS, width), pick),
                pl.BlockSpec((None, ROWS, depth), pick),
                pl.BlockSpec((None, ROWS, depth), pick),
                pl.BlockSpec(y.shape, lambda i, *_: (0, 0)),
            ],
            out_specs=[out_spec(group) for group in range(groups)],
        ),
        out_shape=[jax.ShapeDtypeStruct((length, ROWS, width), z.dtype)] * groups,
    )(blocks, filled, jnp.zeros((1,), jnp.int32) if base is None else base.reshape(1), z, a, b, y)


def settle_kernel(groups, count, slot_ref, owned_ref, *refs):
    z_refs, (v_ref, y_ref, out_ref) = refs[:groups], refs[groups:]
    parts, depth = v_ref.shape[0], v_ref.shape[-1]
    for group in range(groups):

        @pl.when(pl.program_id(0) // count == group)
        def _():
            value = z_refs[group][...].astype(jnp.float32)
            for part in range(parts):
                value = value - jnp.dot(
                    v_ref[part], y_ref[part * depth : (part + 1) * depth, :], preferred_element_type=jnp.float32
                )
            out_ref[...] = value.astype(out_ref.dtype)


def settle_there(owned, z_list, v, y, first, stride, slots):
    groups, count, width = len(z_list), z_list[0].shape[0], owned.shape[2]
    parts, depth = v.shape[0], v.shape[3]

    def z_spec(group):
        return pl.BlockSpec((None, ROWS, width), lambda i, slot_ref: (jnp.clip(i - group * count, 0, count - 1), 0, 0))

    return pl.pallas_call(
        functools.partial(settle_kernel, groups, count),
        grid_spec=pltpu.PrefetchScalarGridSpec(
            num_scalar_prefetch=1,
            grid=(groups * count,),
            in_specs=[pl.BlockSpec(memory_space=pl.ANY)]
            + [z_spec(group) for group in range(groups)]
            + [
                pl.BlockSpec(
                    (parts, None, ROWS, depth),
                    lambda i, slot_ref: (0, (i // count) * stride + first + i % count, 0, 0),
                ),
                pl.BlockSpec(y.shape, lambda i, slot_ref: (0, 0)),
            ],
            out_specs=pl.BlockSpec((None, ROWS, width), lambda i, slot_ref: (slot_ref[i], 0, 0)),
        ),
        out_shape=jax.ShapeDtypeStruct(owned.shape, owned.dtype),
        input_output_aliases={1: 0},
    )(slots, owned, *z_list, v, y)


def relay_kernel(groups, lanes, per_lane, index_ref, filled_ref, *rest):
    sources, rest = rest[:lanes], rest[lanes:]
    outs, (stage, in_sems, out_sems) = rest[:groups], rest[groups:]
    count = lanes * per_lane

    def inward(k):
        return pltpu.make_async_copy(sources[k % count // per_lane].at[index_ref[k]], stage.at[k], in_sems.at[k])

    def outward(k):
        return pltpu.make_async_copy(stage.at[k], outs[k // count].at[k % count], out_sems.at[k])

    for k in range(groups * count):

        @pl.when(filled_ref[k] > 0)
        def _():
            inward(k).start()

    for k in range(groups * count):

        @pl.when(filled_ref[k] > 0)
        def _():
            inward(k).wait()

        @pl.when(filled_ref[k] <= 0)
        def _():
            stage[k] = jnp.zeros(stage.shape[1:], stage.dtype)

        outward(k).start()
    for k in range(groups * count):
        outward(k).wait()


def relay_blocks(sources, index, filled, groups, per_lane):
    any_spec = pl.BlockSpec(memory_space=pl.ANY)
    smem_spec = pl.BlockSpec(memory_space=pltpu.SMEM)
    lanes, block, dtype = len(sources), sources[0].shape[1:], sources[0].dtype
    total = groups * lanes * per_lane
    return pl.pallas_call(
        functools.partial(relay_kernel, groups, lanes, per_lane),
        out_shape=[jax.ShapeDtypeStruct((lanes * per_lane,) + block, dtype)] * groups,
        in_specs=[smem_spec, smem_spec] + [any_spec] * lanes,
        out_specs=[any_spec] * groups,
        scratch_shapes=[
            pltpu.VMEM((total,) + block, dtype),
            pltpu.SemaphoreType.DMA((total,)),
            pltpu.SemaphoreType.DMA((total,)),
        ],
        compiler_params=pltpu.CompilerParams(vmem_limit_bytes=56 * 2**20),
    )(index, filled, *sources)


def fill_kernel(origins, choice_ref, slot_ref, owned_ref, *rest):
    arrays = len(rest) - 4
    sources, (out_ref, stage, in_sems, out_sems) = rest[:arrays], rest[arrays:]
    total = stage.shape[0]
    for k in range(total):
        for option, (array, item) in enumerate(origins[k]):

            @pl.when(choice_ref[k] == option + 1)
            def _():
                pltpu.make_async_copy(sources[array].at[item], stage.at[k], in_sems.at[k]).start()

    for k in range(total):

        @pl.when(choice_ref[k] > 0)
        def _():
            pltpu.make_async_copy(sources[0].at[0], stage.at[k], in_sems.at[k]).wait()

        @pl.when(choice_ref[k] <= 0)
        def _():
            stage[k] = jnp.zeros(stage.shape[1:], stage.dtype)

        pltpu.make_async_copy(stage.at[k], out_ref.at[slot_ref[k]], out_sems.at[k]).start()
    for k in range(total):
        pltpu.make_async_copy(stage.at[k], out_ref.at[slot_ref[k]], out_sems.at[k]).wait()


def fill_slots(owned, sources, origins, choice, slots):
    any_spec = pl.BlockSpec(memory_space=pl.ANY)
    smem_spec = pl.BlockSpec(memory_space=pltpu.SMEM)
    total = len(origins)
    return pl.pallas_call(
        functools.partial(fill_kernel, origins),
        out_shape=jax.ShapeDtypeStruct(owned.shape, owned.dtype),
        in_specs=[smem_spec, smem_spec, any_spec] + [any_spec] * len(sources),
        out_specs=any_spec,
        scratch_shapes=[
            pltpu.VMEM((total,) + owned.shape[1:], owned.dtype),
            pltpu.SemaphoreType.DMA((total,)),
            pltpu.SemaphoreType.DMA((total,)),
        ],
        input_output_aliases={2: 0},
    )(choice, slots, owned, *sources)


def match_spares(counts, low, base, top):
    streams = counts.shape[0]
    spare = ((low + jnp.arange(base - low))[None, :] >= counts[:, None]).reshape(-1).astype(jnp.int32)
    over = ((base + jnp.arange(top - base))[None, :] < counts[:, None]).reshape(-1).astype(jnp.int32)

    def rank(flags):
        k = jnp.arange(flags.shape[0])
        return jnp.sum(flags[None, :] * (k[None, :] < k[:, None]), axis=1)

    hit = spare[:, None] * over[None, :] * (rank(spare)[:, None] == rank(over)[None, :])
    return hit.reshape(streams, base - low, streams, top - base), jnp.sum(over) <= jnp.sum(spare)


def body(eigvecs, reflectors, t_factors, owners, band_owner):
    row_count, col_count = lax.axis_size("row"), lax.axis_size("col")
    me, col = lax.axis_index("row"), lax.axis_index("col")
    block_count = eigvecs.shape[0] // ROWS
    width = eigvecs.shape[1]
    depth = reflectors.shape[1]
    capacity = (5 * block_count + 4 * row_count - 1) // (4 * row_count)
    slot_total = row_count * capacity
    early = 9 * capacity // 20
    base = capacity - capacity // 10
    low = early + max(1, 3 * (capacity - early) // 11)
    share = 2 * depth // col_count
    half = row_count // 2
    near, far = list(range(1, half)), list(range(half, row_count))
    order = near[half // 2 - 1 :] + far + near[: half // 2 - 1]
    early_parts = [(0, max(1, early // 6))]
    early_parts += [(early_parts[0][1], early - early_parts[0][1])]

    owner_of = band_owner[:, 0]
    position = jnp.arange(block_count, dtype=jnp.int32)
    shared = (owner_of[:, None] == owner_of[None, :]) & (position[None, :] < position[:, None])
    order_in = jnp.sum(shared.astype(jnp.int32), axis=1)
    slot_index = owner_of * capacity + order_in
    hits = (slot_index[None, :] == jnp.arange(slot_total, dtype=jnp.int32)[:, None]).astype(jnp.int32)
    slot_table = jnp.stack([jnp.sum(hits * position[None, :], axis=1), jnp.sum(hits, axis=1)])

    counts = jnp.sum((owner_of[:, None] == jnp.arange(row_count)[None, :]).astype(jnp.int32), axis=0)

    def tables(at, count, distances=None):
        starts = [(me ^ d) * capacity + at for d in distances or order]
        both = jnp.concatenate([lax.dynamic_slice(slot_table, (0, s), (2, count)) for s in starts], axis=1)
        return both[0], both[1]

    z = eigvecs.reshape(block_count, ROWS, width)

    raw = {}
    for at, count in early_parts:
        packed = gather_blocks(z, *tables(at, count), len(order), count)
        raw[at] = [swap(item, row_count, d) for d, item in zip(order, packed)]

    candidates = lax.all_gather(reflectors, "col", axis=0)
    panels = [lax.dynamic_index_in_dim(candidates, owners[which], 0, keepdims=False) for which in range(2)]
    mine = jnp.concatenate([jnp.where(col == owners[which], t_factors, 0.0) for which in range(2)], axis=0)
    triangles = lax.psum(mine, "col")

    partial_value = jnp.concatenate(
        [
            lax.dot_general(panel, eigvecs, contract_rows, preferred_element_type=jnp.float32)
            for panel in panels
        ],
        axis=0,
    )
    gram = lax.dot_general(panels[1], panels[0], contract_rows, preferred_element_type=jnp.float32)
    gram = jnp.concatenate([jnp.zeros_like(gram), gram], axis=0)
    partial_value = jnp.concatenate([partial_value.astype(jnp.bfloat16), gram.astype(jnp.bfloat16)], axis=1)
    told = jnp.where(jnp.arange(16 * ((row_count + 15) // 16))[:, None] == me, counts[None, :], 0)
    told = jnp.pad(told.astype(jnp.bfloat16), ((0, 0), (0, width + depth - row_count)))
    totals = lax.psum(jnp.concatenate([partial_value, told], axis=0), "row").astype(jnp.float32)
    products, gram = totals[: 2 * depth, :width], totals[depth : 2 * depth, width:]
    all_counts = totals[2 * depth : 2 * depth + row_count, :row_count].astype(jnp.int32)
    first = jnp.dot(triangles[:depth], products[:depth], precision=lax.Precision.HIGHEST).astype(jnp.bfloat16)
    rest = products[depth:] - jnp.dot(gram, first.astype(jnp.float32), precision=lax.Precision.HIGHEST)
    second = jnp.dot(triangles[depth:], rest, precision=lax.Precision.HIGHEST).astype(jnp.bfloat16)
    update = jnp.concatenate([first, second], axis=0)

    both = jnp.concatenate(panels, axis=1)
    slim = lax.dynamic_slice(both, (0, col * share), (both.shape[0], share)).reshape(block_count, ROWS, share)
    slim_packed = gather_blocks(slim, *tables(0, early), len(order), early)
    slim_list = [swap(item, row_count, d) for d, item in zip(order, slim_packed)]

    v0 = panels[0].reshape(block_count, ROWS, depth)
    v1 = panels[1].reshape(block_count, ROWS, depth)

    overflow = capacity - base
    cross = jnp.stack([lax.dynamic_index_in_dim(counts, me ^ d, 0, keepdims=False) for d in far])
    first_block, first_filled = tables(low, base - low, far)
    if overflow:
        hit, _ = match_spares(cross, low, base, capacity)
        hit = hit.reshape(-1, len(far) * overflow)
        spill_block, _ = tables(base, overflow, far)
        first_block = first_block + jnp.sum(hit * spill_block[None, :], axis=1)
        first_filled = first_filled + jnp.sum(hit, axis=1)

    late = {}
    done = finish_here(z, v0, v1, update, first_block, first_filled, len(far), base - low)
    late["far"] = [swap(item, row_count, d) for d, item in zip(far, done)]
    done = finish_here(z, v0, v1, update, *tables(low, capacity - low, near), len(near), capacity - low)
    late["near"] = [swap(item, row_count, d) for d, item in zip(near, done)]
    done = finish_here(z, v0, v1, update, *tables(early, low - early), len(order), low - early)
    late["last"] = [swap(item, row_count, d) for d, item in zip(order, done)]

    slim_list, _ = lax.optimization_barrier((slim_list, done))
    wide_there = lax.all_gather(jnp.concatenate(slim_list, axis=0), "col", axis=0)

    mine = lax.dynamic_slice(slot_table, (0, me * capacity), (2, capacity))
    (owned,) = finish_here(z, v0, v1, update, mine[0], mine[1], 1, capacity, me * capacity, slot_total)
    for at, count in early_parts:
        slots = jnp.concatenate([(me ^ d) * capacity + at + jnp.arange(count, dtype=jnp.int32) for d in order])
        owned = settle_there(owned, raw[at], wide_there, update, at, early, slots)

    def place(owned, distance, at, value):
        return lax.dynamic_update_slice(owned, value, ((me ^ distance) * capacity + at, 0, 0))

    if overflow:
        pairs = (jnp.arange(row_count)[:, None] ^ jnp.asarray(far)[None, :])[:, :, None] == jnp.arange(row_count)
        crossing = jnp.sum(all_counts[:, None, :] * pairs, axis=2)
        hits, fits = jax.vmap(lambda c: match_spares(c, low, base, capacity))(crossing)
        fits = jnp.all(fits)
        seen = [lax.dynamic_index_in_dim(hits, me ^ d, 0, keepdims=False) for d in far]
        index, filled = [], []
        for d in near:
            for stream in range(len(far)):
                found = seen[stream][stream, :, (far[stream] ^ d) - half, :]
                index.append(jnp.sum(found * jnp.arange(base - low)[:, None], axis=0))
                filled.append(jnp.sum(found, axis=0))
        relayed = relay_blocks(late["far"], jnp.concatenate(index), jnp.concatenate(filled), len(near), overflow)
        relayed = [swap(item, row_count, d) for d, item in zip(near, relayed)]

    for d, item in zip(near, late["near"]):
        owned = place(owned, d, low, item)
    for d, item in zip(far, late["far"]):
        if overflow:
            held = lax.dynamic_index_in_dim(all_counts[:, :], me ^ d, 0, keepdims=False)
            held = lax.dynamic_index_in_dim(held, me, 0, keepdims=False)
            item = jnp.where((low + jnp.arange(base - low) < held)[:, None, None], item, 0).astype(item.dtype)
        owned = place(owned, d, low, item)

    if overflow:
        gate, owned = lax.optimization_barrier((fits, owned))

        def direct():
            sent = finish_here(z, v0, v1, update, *tables(base, overflow, far), len(far), overflow)
            return [swap(item, row_count, d) for d, item in zip(far, sent)]

        def nothing():
            return [jnp.zeros((overflow, ROWS, width), z.dtype)] * len(far)

        straight = lax.cond(gate, nothing, direct)
    for d, item in zip(order, late["last"]):
        owned = place(owned, d, early, item)

    if overflow:
        origins, choice, slots = [], [], []
        for owner, d in enumerate(far):
            for item in range(overflow):
                options, picked = [], 0
                for number, step in enumerate(near):
                    stream = (d ^ step) - half
                    options.append((number, stream * overflow + item))
                    picked = picked + (number + 1) * jnp.sum(seen[owner][stream, :, owner, item])
                options.append((len(near) + owner, item))
                origins.append(tuple(options))
                choice.append(jnp.where(fits, picked, len(options)))
                slots.append((me ^ d) * capacity + base + item)
        owned = fill_slots(owned, relayed + straight, tuple(origins), jnp.stack(choice), jnp.stack(slots))
    return owned.reshape(slot_total * ROWS, width)


def solution(mesh):
    in_specs = (P("row", "col"), P("row", "col"), P("col", None), P(), P("row", None))
    out_specs = P("row", "col")
    return jax.shard_map(body, mesh=mesh, in_specs=in_specs, out_specs=out_specs, check_vma=False)
```

```python
import functools

import jax
import jax.numpy as jnp
from jax import lax
from jax.experimental import pallas as pl
from jax.experimental.pallas import tpu as pltpu
from jax.sharding import PartitionSpec as P


ROWS = 128
contract_rows = (((0,), (0,)), ((), ()))


def swap(value, row_count, distance):
    return lax.ppermute(value, "row", [(s, s ^ distance) for s in range(row_count)])


def gather_kernel(groups, count, block_ref, filled_ref, source, *rest):
    outs, (stage, in_sems, out_sems) = rest[:groups], rest[groups:]

    def inward(k):
        return pltpu.make_async_copy(source.at[block_ref[k]], stage.at[k], in_sems.at[k])

    def fetch(k, carry):
        @pl.when(filled_ref[k] > 0)
        def _():
            inward(k).start()

        return carry

    lax.fori_loop(0, groups * count, fetch, 0)
    for group in range(groups):

        def send(item, carry):
            k = group * count + item

            @pl.when(filled_ref[k] > 0)
            def _():
                inward(k).wait()

            @pl.when(filled_ref[k] <= 0)
            def _():
                stage[k] = jnp.zeros(stage.shape[1:], stage.dtype)

            pltpu.make_async_copy(stage.at[k], outs[group].at[item], out_sems.at[k]).start()
            return carry

        lax.fori_loop(0, count, send, 0)
    for group in range(groups):

        def drain(item, carry):
            k = group * count + item
            pltpu.make_async_copy(stage.at[k], outs[group].at[item], out_sems.at[k]).wait()
            return carry

        lax.fori_loop(0, count, drain, 0)


def gather_blocks(source, blocks, filled, groups, count):
    any_spec = pl.BlockSpec(memory_space=pl.ANY)
    smem_spec = pl.BlockSpec(memory_space=pltpu.SMEM)
    out = jax.ShapeDtypeStruct((count,) + source.shape[1:], source.dtype)
    total = groups * count
    return pl.pallas_call(
        functools.partial(gather_kernel, groups, count),
        out_shape=[out] * groups,
        in_specs=[smem_spec, smem_spec, any_spec],
        out_specs=[any_spec] * groups,
        scratch_shapes=[
            pltpu.VMEM((total,) + source.shape[1:], source.dtype),
            pltpu.SemaphoreType.DMA((total,)),
            pltpu.SemaphoreType.DMA((total,)),
        ],
        compiler_params=pltpu.CompilerParams(vmem_limit_bytes=56 * 2**20),
    )(blocks, filled, source)


def finish_kernel(groups, count, block_ref, filled_ref, base_ref, z_ref, a_ref, b_ref, y_ref, *outs):
    depth = a_ref.shape[-1]
    step = pl.program_id(0)
    value = z_ref[...].astype(jnp.float32)
    value = value - jnp.dot(a_ref[...], y_ref[:depth, :], preferred_element_type=jnp.float32)
    value = value - jnp.dot(b_ref[...], y_ref[depth:, :], preferred_element_type=jnp.float32)
    value = jnp.where(filled_ref[step] > 0, value, 0.0).astype(outs[0].dtype)
    for group in range(groups):

        @pl.when(step // count == group)
        def _():
            outs[group][...] = value


def finish_here(z, a, b, y, blocks, filled, groups, count, base=None, slot_total=None):
    width, depth = z.shape[2], a.shape[2]
    pick = lambda i, block_ref, *_: (block_ref[i], 0, 0)

    def out_spec(group):
        if base is not None:
            return pl.BlockSpec((None, ROWS, width), lambda i, block_ref, filled_ref, base_ref: (base_ref[0] + i, 0, 0))
        return pl.BlockSpec((None, ROWS, width), lambda i, *_: (jnp.clip(i - group * count, 0, count - 1), 0, 0))

    length = count if slot_total is None else slot_total
    return pl.pallas_call(
        functools.partial(finish_kernel, groups, count),
        grid_spec=pltpu.PrefetchScalarGridSpec(
            num_scalar_prefetch=3,
            grid=(groups * count,),
            in_specs=[
                pl.BlockSpec((None, ROWS, width), pick),
                pl.BlockSpec((None, ROWS, depth), pick),
                pl.BlockSpec((None, ROWS, depth), pick),
                pl.BlockSpec(y.shape, lambda i, *_: (0, 0)),
            ],
            out_specs=[out_spec(group) for group in range(groups)],
        ),
        out_shape=[jax.ShapeDtypeStruct((length, ROWS, width), z.dtype)] * groups,
    )(blocks, filled, jnp.zeros((1,), jnp.int32) if base is None else base.reshape(1), z, a, b, y)


def settle_kernel(groups, count, slot_ref, owned_ref, *refs):
    z_refs, (v_ref, y_ref, out_ref) = refs[:groups], refs[groups:]
    parts, depth = v_ref.shape[0], v_ref.shape[-1]
    for group in range(groups):

        @pl.when(pl.program_id(0) // count == group)
        def _():
            value = z_refs[group][...].astype(jnp.float32)
            for part in range(parts):
                value = value - jnp.dot(
                    v_ref[part], y_ref[part * depth : (part + 1) * depth, :], preferred_element_type=jnp.float32
                )
            out_ref[...] = value.astype(out_ref.dtype)


def settle_there(owned, z_list, v, y, first, stride, slots):
    groups, count, width = len(z_list), z_list[0].shape[0], owned.shape[2]
    parts, depth = v.shape[0], v.shape[3]

    def z_spec(group):
        return pl.BlockSpec((None, ROWS, width), lambda i, slot_ref: (jnp.clip(i - group * count, 0, count - 1), 0, 0))

    return pl.pallas_call(
        functools.partial(settle_kernel, groups, count),
        grid_spec=pltpu.PrefetchScalarGridSpec(
            num_scalar_prefetch=1,
            grid=(groups * count,),
            in_specs=[pl.BlockSpec(memory_space=pl.ANY)]
            + [z_spec(group) for group in range(groups)]
            + [
                pl.BlockSpec(
                    (parts, None, ROWS, depth),
                    lambda i, slot_ref: (0, (i // count) * stride + first + i % count, 0, 0),
                ),
                pl.BlockSpec(y.shape, lambda i, slot_ref: (0, 0)),
            ],
            out_specs=pl.BlockSpec((None, ROWS, width), lambda i, slot_ref: (slot_ref[i], 0, 0)),
        ),
        out_shape=jax.ShapeDtypeStruct(owned.shape, owned.dtype),
        input_output_aliases={1: 0},
    )(slots, owned, *z_list, v, y)


def relay_kernel(groups, lanes, per_lane, index_ref, filled_ref, *rest):
    sources, rest = rest[:lanes], rest[lanes:]
    outs, (stage, in_sems, out_sems) = rest[:groups], rest[groups:]
    count = lanes * per_lane

    def inward(k):
        return pltpu.make_async_copy(sources[k % count // per_lane].at[index_ref[k]], stage.at[k], in_sems.at[k])

    def outward(k):
        return pltpu.make_async_copy(stage.at[k], outs[k // count].at[k % count], out_sems.at[k])

    for k in range(groups * count):

        @pl.when(filled_ref[k] > 0)
        def _():
            inward(k).start()

    for k in range(groups * count):

        @pl.when(filled_ref[k] > 0)
        def _():
            inward(k).wait()

        @pl.when(filled_ref[k] <= 0)
        def _():
            stage[k] = jnp.zeros(stage.shape[1:], stage.dtype)

        outward(k).start()
    for k in range(groups * count):
        outward(k).wait()


def relay_blocks(sources, index, filled, groups, per_lane):
    any_spec = pl.BlockSpec(memory_space=pl.ANY)
    smem_spec = pl.BlockSpec(memory_space=pltpu.SMEM)
    lanes, block, dtype = len(sources), sources[0].shape[1:], sources[0].dtype
    total = groups * lanes * per_lane
    return pl.pallas_call(
        functools.partial(relay_kernel, groups, lanes, per_lane),
        out_shape=[jax.ShapeDtypeStruct((lanes * per_lane,) + block, dtype)] * groups,
        in_specs=[smem_spec, smem_spec] + [any_spec] * lanes,
        out_specs=[any_spec] * groups,
        scratch_shapes=[
            pltpu.VMEM((total,) + block, dtype),
            pltpu.SemaphoreType.DMA((total,)),
            pltpu.SemaphoreType.DMA((total,)),
        ],
        compiler_params=pltpu.CompilerParams(vmem_limit_bytes=56 * 2**20),
    )(index, filled, *sources)


def fill_kernel(origins, choice_ref, slot_ref, owned_ref, *rest):
    arrays = len(rest) - 4
    sources, (out_ref, stage, in_sems, out_sems) = rest[:arrays], rest[arrays:]
    total = stage.shape[0]
    for k in range(total):
        for option, (array, item) in enumerate(origins[k]):

            @pl.when(choice_ref[k] == option + 1)
            def _():
                pltpu.make_async_copy(sources[array].at[item], stage.at[k], in_sems.at[k]).start()

    for k in range(total):

        @pl.when(choice_ref[k] > 0)
        def _():
            pltpu.make_async_copy(sources[0].at[0], stage.at[k], in_sems.at[k]).wait()

        @pl.when(choice_ref[k] <= 0)
        def _():
            stage[k] = jnp.zeros(stage.shape[1:], stage.dtype)

        pltpu.make_async_copy(stage.at[k], out_ref.at[slot_ref[k]], out_sems.at[k]).start()
    for k in range(total):
        pltpu.make_async_copy(stage.at[k], out_ref.at[slot_ref[k]], out_sems.at[k]).wait()


def fill_slots(owned, sources, origins, choice, slots):
    any_spec = pl.BlockSpec(memory_space=pl.ANY)
    smem_spec = pl.BlockSpec(memory_space=pltpu.SMEM)
    total = len(origins)
    return pl.pallas_call(
        functools.partial(fill_kernel, origins),
        out_shape=jax.ShapeDtypeStruct(owned.shape, owned.dtype),
        in_specs=[smem_spec, smem_spec, any_spec] + [any_spec] * len(sources),
        out_specs=any_spec,
        scratch_shapes=[
            pltpu.VMEM((total,) + owned.shape[1:], owned.dtype),
            pltpu.SemaphoreType.DMA((total,)),
            pltpu.SemaphoreType.DMA((total,)),
        ],
        input_output_aliases={2: 0},
    )(choice, slots, owned, *sources)


def match_spares(counts, low, base, top):
    streams = counts.shape[0]
    spare = ((low + jnp.arange(base - low))[None, :] >= counts[:, None]).reshape(-1).astype(jnp.int32)
    over = ((base + jnp.arange(top - base))[None, :] < counts[:, None]).reshape(-1).astype(jnp.int32)

    def rank(flags):
        k = jnp.arange(flags.shape[0])
        return jnp.sum(flags[None, :] * (k[None, :] < k[:, None]), axis=1)

    hit = spare[:, None] * over[None, :] * (rank(spare)[:, None] == rank(over)[None, :])
    return hit.reshape(streams, base - low, streams, top - base), jnp.sum(over) <= jnp.sum(spare)


def body(eigvecs, reflectors, t_factors, owners, band_owner):
    row_count, col_count = lax.axis_size("row"), lax.axis_size("col")
    me, col = lax.axis_index("row"), lax.axis_index("col")
    block_count = eigvecs.shape[0] // ROWS
    width = eigvecs.shape[1]
    depth = reflectors.shape[1]
    capacity = (5 * block_count + 4 * row_count - 1) // (4 * row_count)
    slot_total = row_count * capacity
    early = 9 * capacity // 20
    base = capacity - capacity // 10
    low = early + max(1, 3 * (capacity - early) // 11)
    share = 2 * depth // col_count
    half = row_count // 2
    near, far = list(range(1, half)), list(range(half, row_count))
    order = near[half // 2 - 1 :] + far + near[: half // 2 - 1]
    classes = ((near, low), (far, early))

    owner_of = band_owner[:, 0]
    position = jnp.arange(block_count, dtype=jnp.int32)
    shared = (owner_of[:, None] == owner_of[None, :]) & (position[None, :] < position[:, None])
    order_in = jnp.sum(shared.astype(jnp.int32), axis=1)
    slot_index = owner_of * capacity + order_in
    hits = (slot_index[None, :] == jnp.arange(slot_total, dtype=jnp.int32)[:, None]).astype(jnp.int32)
    slot_table = jnp.stack([jnp.sum(hits * position[None, :], axis=1), jnp.sum(hits, axis=1)])

    counts = jnp.sum((owner_of[:, None] == jnp.arange(row_count)[None, :]).astype(jnp.int32), axis=0)

    def tables(at, count, distances=None):
        starts = [(me ^ d) * capacity + at for d in distances or order]
        both = jnp.concatenate([lax.dynamic_slice(slot_table, (0, s), (2, count)) for s in starts], axis=1)
        return both[0], both[1]

    z = eigvecs.reshape(block_count, ROWS, width)

    lead = max(1, early // 6)
    raw = {}
    packed = gather_blocks(z, *tables(0, lead), len(order), lead)
    moved = {d: swap(item, row_count, d) for d, item in zip(order, packed)}
    for number, (distances, until) in enumerate(classes):
        raw[number] = [(0, lead, [moved[d] for d in distances])]
    for number, (distances, until) in reversed(list(enumerate(classes))):
        count = until - lead
        if count:
            packed = gather_blocks(z, *tables(lead, count, distances), len(distances), count)
            packed = [swap(item, row_count, d) for d, item in zip(distances, packed)]
            raw[number].append((lead, count, packed))

    candidates = lax.all_gather(reflectors, "col", axis=0)
    panels = [lax.dynamic_index_in_dim(candidates, owners[which], 0, keepdims=False) for which in range(2)]
    mine = jnp.concatenate([jnp.where(col == owners[which], t_factors, 0.0) for which in range(2)], axis=0)
    triangles = lax.psum(mine, "col")

    partial_value = jnp.concatenate(
        [
            lax.dot_general(panel, eigvecs, contract_rows, preferred_element_type=jnp.float32)
            for panel in panels
        ],
        axis=0,
    )
    gram = lax.dot_general(panels[1], panels[0], contract_rows, preferred_element_type=jnp.float32)
    gram = jnp.concatenate([jnp.zeros_like(gram), gram], axis=0)
    partial_value = jnp.concatenate([partial_value.astype(jnp.bfloat16), gram.astype(jnp.bfloat16)], axis=1)
    told = jnp.where(jnp.arange(16 * ((row_count + 15) // 16))[:, None] == me, counts[None, :], 0)
    told = jnp.pad(told.astype(jnp.bfloat16), ((0, 0), (0, width + depth - row_count)))
    totals = lax.psum(jnp.concatenate([partial_value, told], axis=0), "row").astype(jnp.float32)
    products, gram = totals[: 2 * depth, :width], totals[depth : 2 * depth, width:]
    all_counts = totals[2 * depth : 2 * depth + row_count, :row_count].astype(jnp.int32)
    first = jnp.dot(triangles[:depth], products[:depth], precision=lax.Precision.HIGHEST).astype(jnp.bfloat16)
    rest = products[depth:] - jnp.dot(gram, first.astype(jnp.float32), precision=lax.Precision.HIGHEST)
    second = jnp.dot(triangles[depth:], rest, precision=lax.Precision.HIGHEST).astype(jnp.bfloat16)
    update = jnp.concatenate([first, second], axis=0)

    both = jnp.concatenate(panels, axis=1)
    slim = lax.dynamic_slice(both, (0, col * share), (both.shape[0], share)).reshape(block_count, ROWS, share)
    slim_list = []
    for distances, until in classes:
        slim_packed = gather_blocks(slim, *tables(0, until, distances), len(distances), until)
        slim_list += [swap(item, row_count, d) for d, item in zip(distances, slim_packed)]

    v0 = panels[0].reshape(block_count, ROWS, depth)
    v1 = panels[1].reshape(block_count, ROWS, depth)

    overflow = capacity - base
    cross = jnp.stack([lax.dynamic_index_in_dim(counts, me ^ d, 0, keepdims=False) for d in far])
    first_block, first_filled = tables(low, base - low, far)
    if overflow:
        hit, _ = match_spares(cross, low, base, capacity)
        hit = hit.reshape(-1, len(far) * overflow)
        spill_block, _ = tables(base, overflow, far)
        first_block = first_block + jnp.sum(hit * spill_block[None, :], axis=1)
        first_filled = first_filled + jnp.sum(hit, axis=1)

    late = {}
    done = finish_here(z, v0, v1, update, first_block, first_filled, len(far), base - low)
    late["far"] = [swap(item, row_count, d) for d, item in zip(far, done)]
    done = finish_here(z, v0, v1, update, *tables(low, capacity - low, near), len(near), capacity - low)
    late["near"] = [swap(item, row_count, d) for d, item in zip(near, done)]
    done = finish_here(z, v0, v1, update, *tables(early, low - early, far), len(far), low - early)
    late["last"] = [swap(item, row_count, d) for d, item in zip(far, done)]

    slim_list, _ = lax.optimization_barrier((slim_list, done))
    wide_there = lax.all_gather(jnp.concatenate(slim_list, axis=0), "col", axis=0)

    mine = lax.dynamic_slice(slot_table, (0, me * capacity), (2, capacity))
    (owned,) = finish_here(z, v0, v1, update, mine[0], mine[1], 1, capacity, me * capacity, slot_total)
    offset = 0
    for number, (distances, until) in enumerate(classes):
        for at, count, items in raw[number]:
            slots = [(me ^ d) * capacity + at + jnp.arange(count, dtype=jnp.int32) for d in distances]
            owned = settle_there(
                owned, items, wide_there, update, offset + at, until, jnp.concatenate(slots)
            )
        offset += len(distances) * until

    def place(owned, distance, at, value):
        return lax.dynamic_update_slice(owned, value, ((me ^ distance) * capacity + at, 0, 0))

    if overflow:
        pairs = (jnp.arange(row_count)[:, None] ^ jnp.asarray(far)[None, :])[:, :, None] == jnp.arange(row_count)
        crossing = jnp.sum(all_counts[:, None, :] * pairs, axis=2)
        hits, fits = jax.vmap(lambda c: match_spares(c, low, base, capacity))(crossing)
        fits = jnp.all(fits)
        seen = [lax.dynamic_index_in_dim(hits, me ^ d, 0, keepdims=False) for d in far]
        lanes = len(far) // 2
        relayed = []
        for part in range(2):
            index, filled = [], []
            for d in near:
                for stream in range(part * lanes, (part + 1) * lanes):
                    found = seen[stream][stream, :, (far[stream] ^ d) - half, :]
                    index.append(jnp.sum(found * jnp.arange(base - low)[:, None], axis=0))
                    filled.append(jnp.sum(found, axis=0))
            sent = relay_blocks(
                late["far"][part * lanes : (part + 1) * lanes],
                jnp.concatenate(index),
                jnp.concatenate(filled),
                len(near),
                overflow,
            )
            relayed += [swap(item, row_count, d) for d, item in zip(near, sent)]

    for d, item in zip(near, late["near"]):
        owned = place(owned, d, low, item)
    for d, item in zip(far, late["far"]):
        if overflow:
            held = lax.dynamic_index_in_dim(all_counts[:, :], me ^ d, 0, keepdims=False)
            held = lax.dynamic_index_in_dim(held, me, 0, keepdims=False)
            item = jnp.where((low + jnp.arange(base - low) < held)[:, None, None], item, 0).astype(item.dtype)
        owned = place(owned, d, low, item)

    if overflow:
        gate, owned = lax.optimization_barrier((fits, owned))

        def direct():
            sent = finish_here(z, v0, v1, update, *tables(base, overflow, far), len(far), overflow)
            return [swap(item, row_count, d) for d, item in zip(far, sent)]

        def nothing():
            return [jnp.zeros((overflow, ROWS, width), z.dtype)] * len(far)

        straight = lax.cond(gate, nothing, direct)
    for d, item in zip(far, late["last"]):
        owned = place(owned, d, early, item)

    if overflow:
        origins, choice, slots = [], [], []
        for owner, d in enumerate(far):
            for item in range(overflow):
                options, picked = [], 0
                for number, step in enumerate(near):
                    stream = (d ^ step) - half
                    options.append((stream // lanes * len(near) + number, stream % lanes * overflow + item))
                    picked = picked + (number + 1) * jnp.sum(seen[owner][stream, :, owner, item])
                options.append((len(relayed) + owner, item))
                origins.append(tuple(options))
                choice.append(jnp.where(fits, picked, len(options)))
                slots.append((me ^ d) * capacity + base + item)
        owned = fill_slots(owned, relayed + straight, tuple(origins), jnp.stack(choice), jnp.stack(slots))
    return owned.reshape(slot_total * ROWS, width)


def solution(mesh):
    in_specs = (P("row", "col"), P("row", "col"), P("col", None), P(), P("row", None))
    out_specs = P("row", "col")
    return jax.shard_map(body, mesh=mesh, in_specs=in_specs, out_specs=out_specs, check_vma=False)
```

```python
import functools

import jax
import jax.numpy as jnp
from jax import lax
from jax.experimental import pallas as pl
from jax.experimental.pallas import tpu as pltpu
from jax.sharding import PartitionSpec as P


ROWS = 128
contract_rows = (((0,), (0,)), ((), ()))


def swap(value, row_count, distance):
    return lax.ppermute(value, "row", [(s, s ^ distance) for s in range(row_count)])


def gather_kernel(groups, count, block_ref, filled_ref, source, *rest):
    outs, (stage, in_sems, out_sems) = rest[:groups], rest[groups:]

    def inward(k):
        return pltpu.make_async_copy(source.at[block_ref[k]], stage.at[k], in_sems.at[k])

    def fetch(k, carry):
        @pl.when(filled_ref[k] > 0)
        def _():
            inward(k).start()

        return carry

    lax.fori_loop(0, groups * count, fetch, 0)
    for group in range(groups):

        def send(item, carry):
            k = group * count + item

            @pl.when(filled_ref[k] > 0)
            def _():
                inward(k).wait()

            @pl.when(filled_ref[k] <= 0)
            def _():
                stage[k] = jnp.zeros(stage.shape[1:], stage.dtype)

            pltpu.make_async_copy(stage.at[k], outs[group].at[item], out_sems.at[k]).start()
            return carry

        lax.fori_loop(0, count, send, 0)
    for group in range(groups):

        def drain(item, carry):
            k = group * count + item
            pltpu.make_async_copy(stage.at[k], outs[group].at[item], out_sems.at[k]).wait()
            return carry

        lax.fori_loop(0, count, drain, 0)


def gather_blocks(source, blocks, filled, groups, count):
    any_spec = pl.BlockSpec(memory_space=pl.ANY)
    smem_spec = pl.BlockSpec(memory_space=pltpu.SMEM)
    out = jax.ShapeDtypeStruct((count,) + source.shape[1:], source.dtype)
    total = groups * count
    return pl.pallas_call(
        functools.partial(gather_kernel, groups, count),
        out_shape=[out] * groups,
        in_specs=[smem_spec, smem_spec, any_spec],
        out_specs=[any_spec] * groups,
        scratch_shapes=[
            pltpu.VMEM((total,) + source.shape[1:], source.dtype),
            pltpu.SemaphoreType.DMA((total,)),
            pltpu.SemaphoreType.DMA((total,)),
        ],
        compiler_params=pltpu.CompilerParams(vmem_limit_bytes=56 * 2**20),
    )(blocks, filled, source)


def finish_kernel(groups, count, block_ref, filled_ref, base_ref, z_ref, a_ref, b_ref, y_ref, *outs):
    depth = a_ref.shape[-1]
    step = pl.program_id(0)
    value = z_ref[...].astype(jnp.float32)
    value = value - jnp.dot(a_ref[...], y_ref[:depth, :], preferred_element_type=jnp.float32)
    value = value - jnp.dot(b_ref[...], y_ref[depth:, :], preferred_element_type=jnp.float32)
    value = jnp.where(filled_ref[step] > 0, value, 0.0).astype(outs[0].dtype)
    for group in range(groups):

        @pl.when(step // count == group)
        def _():
            outs[group][...] = value


def finish_here(z, a, b, y, blocks, filled, groups, count, base=None, slot_total=None):
    width, depth = z.shape[2], a.shape[2]
    pick = lambda i, block_ref, *_: (block_ref[i], 0, 0)

    def out_spec(group):
        if base is not None:
            return pl.BlockSpec((None, ROWS, width), lambda i, block_ref, filled_ref, base_ref: (base_ref[0] + i, 0, 0))
        return pl.BlockSpec((None, ROWS, width), lambda i, *_: (jnp.clip(i - group * count, 0, count - 1), 0, 0))

    length = count if slot_total is None else slot_total
    return pl.pallas_call(
        functools.partial(finish_kernel, groups, count),
        grid_spec=pltpu.PrefetchScalarGridSpec(
            num_scalar_prefetch=3,
            grid=(groups * count,),
            in_specs=[
                pl.BlockSpec((None, ROWS, width), pick),
                pl.BlockSpec((None, ROWS, depth), pick),
                pl.BlockSpec((None, ROWS, depth), pick),
                pl.BlockSpec(y.shape, lambda i, *_: (0, 0)),
            ],
            out_specs=[out_spec(group) for group in range(groups)],
        ),
        out_shape=[jax.ShapeDtypeStruct((length, ROWS, width), z.dtype)] * groups,
    )(blocks, filled, jnp.zeros((1,), jnp.int32) if base is None else base.reshape(1), z, a, b, y)


def settle_kernel(groups, count, slot_ref, owned_ref, *refs):
    z_refs, (v_ref, y_ref, out_ref) = refs[:groups], refs[groups:]
    parts, depth = v_ref.shape[0], v_ref.shape[-1]
    for group in range(groups):

        @pl.when(pl.program_id(0) // count == group)
        def _():
            value = z_refs[group][...].astype(jnp.float32)
            for part in range(parts):
                value = value - jnp.dot(
                    v_ref[part], y_ref[part * depth : (part + 1) * depth, :], preferred_element_type=jnp.float32
                )
            out_ref[...] = value.astype(out_ref.dtype)


def settle_there(owned, z_list, v, y, first, stride, slots):
    groups, count, width = len(z_list), z_list[0].shape[0], owned.shape[2]
    parts, depth = v.shape[0], v.shape[3]

    def z_spec(group):
        return pl.BlockSpec((None, ROWS, width), lambda i, slot_ref: (jnp.clip(i - group * count, 0, count - 1), 0, 0))

    return pl.pallas_call(
        functools.partial(settle_kernel, groups, count),
        grid_spec=pltpu.PrefetchScalarGridSpec(
            num_scalar_prefetch=1,
            grid=(groups * count,),
            in_specs=[pl.BlockSpec(memory_space=pl.ANY)]
            + [z_spec(group) for group in range(groups)]
            + [
                pl.BlockSpec(
                    (parts, None, ROWS, depth),
                    lambda i, slot_ref: (0, (i // count) * stride + first + i % count, 0, 0),
                ),
                pl.BlockSpec(y.shape, lambda i, slot_ref: (0, 0)),
            ],
            out_specs=pl.BlockSpec((None, ROWS, width), lambda i, slot_ref: (slot_ref[i], 0, 0)),
        ),
        out_shape=jax.ShapeDtypeStruct(owned.shape, owned.dtype),
        input_output_aliases={1: 0},
    )(slots, owned, *z_list, v, y)


def relay_kernel(groups, lanes, per_lane, index_ref, filled_ref, *rest):
    sources, rest = rest[:lanes], rest[lanes:]
    outs, (stage, in_sems, out_sems) = rest[:groups], rest[groups:]
    count = lanes * per_lane

    def inward(k):
        return pltpu.make_async_copy(sources[k % count // per_lane].at[index_ref[k]], stage.at[k], in_sems.at[k])

    def outward(k):
        return pltpu.make_async_copy(stage.at[k], outs[k // count].at[k % count], out_sems.at[k])

    for k in range(groups * count):

        @pl.when(filled_ref[k] > 0)
        def _():
            inward(k).start()

    for k in range(groups * count):

        @pl.when(filled_ref[k] > 0)
        def _():
            inward(k).wait()

        @pl.when(filled_ref[k] <= 0)
        def _():
            stage[k] = jnp.zeros(stage.shape[1:], stage.dtype)

        outward(k).start()
    for k in range(groups * count):
        outward(k).wait()


def relay_blocks(sources, index, filled, groups, per_lane):
    any_spec = pl.BlockSpec(memory_space=pl.ANY)
    smem_spec = pl.BlockSpec(memory_space=pltpu.SMEM)
    lanes, block, dtype = len(sources), sources[0].shape[1:], sources[0].dtype
    total = groups * lanes * per_lane
    return pl.pallas_call(
        functools.partial(relay_kernel, groups, lanes, per_lane),
        out_shape=[jax.ShapeDtypeStruct((lanes * per_lane,) + block, dtype)] * groups,
        in_specs=[smem_spec, smem_spec] + [any_spec] * lanes,
        out_specs=[any_spec] * groups,
        scratch_shapes=[
            pltpu.VMEM((total,) + block, dtype),
            pltpu.SemaphoreType.DMA((total,)),
            pltpu.SemaphoreType.DMA((total,)),
        ],
        compiler_params=pltpu.CompilerParams(vmem_limit_bytes=56 * 2**20),
    )(index, filled, *sources)


def fill_kernel(origins, choice_ref, slot_ref, owned_ref, *rest):
    arrays = len(rest) - 4
    sources, (out_ref, stage, in_sems, out_sems) = rest[:arrays], rest[arrays:]
    total = stage.shape[0]
    for k in range(total):
        for option, (array, item) in enumerate(origins[k]):

            @pl.when(choice_ref[k] == option + 1)
            def _():
                pltpu.make_async_copy(sources[array].at[item], stage.at[k], in_sems.at[k]).start()

    for k in range(total):

        @pl.when(choice_ref[k] > 0)
        def _():
            pltpu.make_async_copy(sources[0].at[0], stage.at[k], in_sems.at[k]).wait()

        @pl.when(choice_ref[k] <= 0)
        def _():
            stage[k] = jnp.zeros(stage.shape[1:], stage.dtype)

        pltpu.make_async_copy(stage.at[k], out_ref.at[slot_ref[k]], out_sems.at[k]).start()
    for k in range(total):
        pltpu.make_async_copy(stage.at[k], out_ref.at[slot_ref[k]], out_sems.at[k]).wait()


def fill_slots(owned, sources, origins, choice, slots):
    any_spec = pl.BlockSpec(memory_space=pl.ANY)
    smem_spec = pl.BlockSpec(memory_space=pltpu.SMEM)
    total = len(origins)
    return pl.pallas_call(
        functools.partial(fill_kernel, origins),
        out_shape=jax.ShapeDtypeStruct(owned.shape, owned.dtype),
        in_specs=[smem_spec, smem_spec, any_spec] + [any_spec] * len(sources),
        out_specs=any_spec,
        scratch_shapes=[
            pltpu.VMEM((total,) + owned.shape[1:], owned.dtype),
            pltpu.SemaphoreType.DMA((total,)),
            pltpu.SemaphoreType.DMA((total,)),
        ],
        input_output_aliases={2: 0},
    )(choice, slots, owned, *sources)


def match_spares(counts, low, base, top):
    streams = counts.shape[0]
    spare = ((low + jnp.arange(base - low))[None, :] >= counts[:, None]).reshape(-1).astype(jnp.int32)
    over = ((base + jnp.arange(top - base))[None, :] < counts[:, None]).reshape(-1).astype(jnp.int32)

    def rank(flags):
        k = jnp.arange(flags.shape[0])
        return jnp.sum(flags[None, :] * (k[None, :] < k[:, None]), axis=1)

    hit = spare[:, None] * over[None, :] * (rank(spare)[:, None] == rank(over)[None, :])
    return hit.reshape(streams, base - low, streams, top - base), jnp.sum(over) <= jnp.sum(spare)


def body(eigvecs, reflectors, t_factors, owners, band_owner):
    row_count, col_count = lax.axis_size("row"), lax.axis_size("col")
    me, col = lax.axis_index("row"), lax.axis_index("col")
    block_count = eigvecs.shape[0] // ROWS
    width = eigvecs.shape[1]
    depth = reflectors.shape[1]
    capacity = (5 * block_count + 4 * row_count - 1) // (4 * row_count)
    slot_total = row_count * capacity
    early = 9 * capacity // 20
    base = capacity - capacity // 10
    low = early + max(1, 3 * (capacity - early) // 11)
    share = 2 * depth // col_count
    half = row_count // 2
    near, far = list(range(1, half)), list(range(half, row_count))
    order = near[half // 2 - 1 :] + far + near[: half // 2 - 1]
    classes = ((near, low), (far, early))

    owner_of = band_owner[:, 0]
    position = jnp.arange(block_count, dtype=jnp.int32)
    shared = (owner_of[:, None] == owner_of[None, :]) & (position[None, :] < position[:, None])
    order_in = jnp.sum(shared.astype(jnp.int32), axis=1)
    slot_index = owner_of * capacity + order_in
    hits = (slot_index[None, :] == jnp.arange(slot_total, dtype=jnp.int32)[:, None]).astype(jnp.int32)
    slot_table = jnp.stack([jnp.sum(hits * position[None, :], axis=1), jnp.sum(hits, axis=1)])

    counts = jnp.sum((owner_of[:, None] == jnp.arange(row_count)[None, :]).astype(jnp.int32), axis=0)

    def tables(at, count, distances=None):
        starts = [(me ^ d) * capacity + at for d in distances or order]
        both = jnp.concatenate([lax.dynamic_slice(slot_table, (0, s), (2, count)) for s in starts], axis=1)
        return both[0], both[1]

    z = eigvecs.reshape(block_count, ROWS, width)

    lead = max(1, early // 6)
    raw = {}
    packed = gather_blocks(z, *tables(0, lead), len(order), lead)
    moved = {d: swap(item, row_count, d) for d, item in zip(order, packed)}
    for number, (distances, until) in enumerate(classes):
        raw[number] = [(0, lead, [moved[d] for d in distances])]
    for number, (distances, until) in reversed(list(enumerate(classes))):
        count = until - lead
        if count:
            packed = gather_blocks(z, *tables(lead, count, distances), len(distances), count)
            packed = [swap(item, row_count, d) for d, item in zip(distances, packed)]
            raw[number].append((lead, count, packed))

    candidates = lax.all_gather(reflectors, "col", axis=0)
    panels = [lax.dynamic_index_in_dim(candidates, owners[which], 0, keepdims=False) for which in range(2)]
    mine = jnp.concatenate([jnp.where(col == owners[which], t_factors, 0.0) for which in range(2)], axis=0)
    triangles = lax.psum(mine, "col")

    partial_value = jnp.concatenate(
        [
            lax.dot_general(panel, eigvecs, contract_rows, preferred_element_type=jnp.float32)
            for panel in panels
        ],
        axis=0,
    )
    gram = lax.dot_general(panels[1], panels[0], contract_rows, preferred_element_type=jnp.float32)
    gram = jnp.concatenate([jnp.zeros_like(gram), gram], axis=0)
    partial_value = jnp.concatenate([partial_value.astype(jnp.bfloat16), gram.astype(jnp.bfloat16)], axis=1)
    told = jnp.where(jnp.arange(16 * ((row_count + 15) // 16))[:, None] == me, counts[None, :], 0)
    told = jnp.pad(told.astype(jnp.bfloat16), ((0, 0), (0, width + depth - row_count)))
    totals = lax.psum(jnp.concatenate([partial_value, told], axis=0), "row").astype(jnp.float32)
    products, gram = totals[: 2 * depth, :width], totals[depth : 2 * depth, width:]
    all_counts = totals[2 * depth : 2 * depth + row_count, :row_count].astype(jnp.int32)
    first = jnp.dot(triangles[:depth], products[:depth], precision=lax.Precision.HIGHEST).astype(jnp.bfloat16)
    rest = products[depth:] - jnp.dot(gram, first.astype(jnp.float32), precision=lax.Precision.HIGHEST)
    second = jnp.dot(triangles[depth:], rest, precision=lax.Precision.HIGHEST).astype(jnp.bfloat16)
    update = jnp.concatenate([first, second], axis=0)

    both = jnp.concatenate(panels, axis=1)
    slim = lax.dynamic_slice(both, (0, col * share), (both.shape[0], share)).reshape(block_count, ROWS, share)
    slim_list = []
    for distances, until in classes:
        slim_packed = gather_blocks(slim, *tables(0, until, distances), len(distances), until)
        slim_list += [swap(item, row_count, d) for d, item in zip(distances, slim_packed)]

    v0 = panels[0].reshape(block_count, ROWS, depth)
    v1 = panels[1].reshape(block_count, ROWS, depth)

    overflow = capacity - base
    cross = jnp.stack([lax.dynamic_index_in_dim(counts, me ^ d, 0, keepdims=False) for d in far])
    first_block, first_filled = tables(low, base - low, far)
    if overflow:
        hit, _ = match_spares(cross, low, base, capacity)
        hit = hit.reshape(-1, len(far) * overflow)
        spill_block, _ = tables(base, overflow, far)
        first_block = first_block + jnp.sum(hit * spill_block[None, :], axis=1)
        first_filled = first_filled + jnp.sum(hit, axis=1)

    late = {}
    done = finish_here(z, v0, v1, update, first_block, first_filled, len(far), base - low)
    late["far"] = [swap(item, row_count, d) for d, item in zip(far, done)]
    done = finish_here(z, v0, v1, update, *tables(low, capacity - low, near), len(near), capacity - low)
    late["near"] = [swap(item, row_count, d) for d, item in zip(near, done)]
    done = finish_here(z, v0, v1, update, *tables(early, low - early, far), len(far), low - early)
    late["last"] = [swap(item, row_count, d) for d, item in zip(far, done)]

    slim_list, _ = lax.optimization_barrier((slim_list, done))
    wide_there = lax.all_gather(jnp.concatenate(slim_list, axis=0), "col", axis=0)

    mine = lax.dynamic_slice(slot_table, (0, me * capacity), (2, capacity))
    (owned,) = finish_here(z, v0, v1, update, mine[0], mine[1], 1, capacity, me * capacity, slot_total)
    offset = 0
    for number, (distances, until) in enumerate(classes):
        for at, count, items in raw[number]:
            slots = [(me ^ d) * capacity + at + jnp.arange(count, dtype=jnp.int32) for d in distances]
            owned = settle_there(
                owned, items, wide_there, update, offset + at, until, jnp.concatenate(slots)
            )
        offset += len(distances) * until

    def place(owned, distance, at, value):
        return lax.dynamic_update_slice(owned, value, ((me ^ distance) * capacity + at, 0, 0))

    if overflow:
        pairs = (jnp.arange(row_count)[:, None] ^ jnp.asarray(far)[None, :])[:, :, None] == jnp.arange(row_count)
        crossing = jnp.sum(all_counts[:, None, :] * pairs, axis=2)
        hits, fits = jax.vmap(lambda c: match_spares(c, low, base, capacity))(crossing)
        fits = jnp.all(fits)
        seen = [lax.dynamic_index_in_dim(hits, me ^ d, 0, keepdims=False) for d in far]
        cut = len(far) - max(1, len(far) // 4)
        relayed = []
        for part, (start, stop) in enumerate(((0, cut), (cut, len(far)))):
            index, filled = [], []
            for d in near:
                for stream in range(start, stop):
                    found = seen[stream][stream, :, (far[stream] ^ d) - half, :]
                    index.append(jnp.sum(found * jnp.arange(base - low)[:, None], axis=0))
                    filled.append(jnp.sum(found, axis=0))
            sent = relay_blocks(
                late["far"][start:stop],
                jnp.concatenate(index),
                jnp.concatenate(filled),
                len(near),
                overflow,
            )
            relayed += [swap(item, row_count, d) for d, item in zip(near, sent)]

    for d, item in zip(near, late["near"]):
        owned = place(owned, d, low, item)
    for d, item in zip(far, late["far"]):
        if overflow:
            held = lax.dynamic_index_in_dim(all_counts[:, :], me ^ d, 0, keepdims=False)
            held = lax.dynamic_index_in_dim(held, me, 0, keepdims=False)
            item = jnp.where((low + jnp.arange(base - low) < held)[:, None, None], item, 0).astype(item.dtype)
        owned = place(owned, d, low, item)

    if overflow:
        gate, owned = lax.optimization_barrier((fits, owned))

        def direct():
            sent = finish_here(z, v0, v1, update, *tables(base, overflow, far), len(far), overflow)
            return [swap(item, row_count, d) for d, item in zip(far, sent)]

        def nothing():
            return [jnp.zeros((overflow, ROWS, width), z.dtype)] * len(far)

        straight = lax.cond(gate, nothing, direct)
    for d, item in zip(far, late["last"]):
        owned = place(owned, d, early, item)

    if overflow:
        origins, choice, slots = [], [], []
        for owner, d in enumerate(far):
            for item in range(overflow):
                options, picked = [], 0
                for number, step in enumerate(near):
                    stream = (d ^ step) - half
                    part, lane = (0, stream) if stream < cut else (1, stream - cut)
                    options.append((part * len(near) + number, lane * overflow + item))
                    picked = picked + (number + 1) * jnp.sum(seen[owner][stream, :, owner, item])
                options.append((len(relayed) + owner, item))
                origins.append(tuple(options))
                choice.append(jnp.where(fits, picked, len(options)))
                slots.append((me ^ d) * capacity + base + item)
        owned = fill_slots(owned, relayed + straight, tuple(origins), jnp.stack(choice), jnp.stack(slots))
    return owned.reshape(slot_total * ROWS, width)


def solution(mesh):
    in_specs = (P("row", "col"), P("row", "col"), P("col", None), P(), P("row", None))
    out_specs = P("row", "col")
    return jax.shard_map(body, mesh=mesh, in_specs=in_specs, out_specs=out_specs, check_vma=False)
```
